32 devices in a mesh: row: 4 (over z), col: 8 (over y, x, core).
Axes of the slice: x: 2, y: 2, z: 4, core: 2. Of those that a mesh axis runs over, the one named last changes fastest.
Arguments:
- inverse_block: float32 [3072, 3072], P('row', 'col'), may hold values from -0.28867513 to 0.28867513, as said below
- grid_position: int32 [3072], replicated, may hold values from 0 to 3071, each once
- panel_a: float32 [512, 3072], P('row', 'col'), may hold values from -1.5 to 1.5
- pivot_inverse_a: float32 [512, 512], replicated, may hold values from -6 to 6
- chosen_rows: int32 [2048], replicated, may hold values from 0 to 3071, as said below
- top_panel_b: float32 [512, 512], replicated, may hold values from -1.5 to 1.5
- panel_b: float32 [512, 2048], P('row', 'col'), may hold values from -1.5 to 1.5
- pivot_inverse_b: float32 [512, 512], replicated, may hold values from -6 to 6
Outputs:
- inverse_panel_a: float32 [3072, 512], P(('row', 'col'))
- diagonal_a: float32 [512, 512], replicated
- inverse_panel_b: float32 [3072, 512], P(('row', 'col'))
- inverse_top_b: float32 [512, 512], replicated
- diagonal_b: float32 [512, 512], replicated
The draws below stay inside these ranges and needn't reach their ends.
Inputs may be any that keep to these rules, and one draw needn't show every extreme that they name: `grid_position`: each of 0 to 3071 appears once. `chosen_rows`: 2048 distinct values. `inverse_block`: symmetric: entry (i, j) equals entry (j, i) in grid storage order.
All inputs are finite; a program needn't handle non-finite values.
Results may differ from the reference program's by a relative error of at most 0.00008.
Values sent between devices are 32-bit elements; how exact they have to be, the bound alone decides.
No kernel may reach another device: no remote copies, remote signals or barrier semaphores. Data moves between devices by JAX's collectives and lax.ppermute only.
A program may use at most 128 MiB of HBM per device.

```python
import jax
import jax.numpy as jnp
from jax import lax

W = 512
M = 3072
MB = 2048
N_ROW = 4
N_COL = 8


def draw_chosen_rows(key, part):
    return jax.random.permutation(jax.random.fold_in(key, 11), M)[:MB].astype(jnp.int32)


def draw_inverse_block(key, part):
    base_key = jax.random.fold_in(key, 23)
    value_key = jax.random.fold_in(base_key, 1)
    pair_key = jax.random.fold_in(base_key, 3)
    groups = N_ROW * N_COL
    tile = M // groups
    values = jax.random.normal(value_key, (M, M), jnp.float32)
    values = (values + values.T) * 0.70710678
    pairing = jax.random.permutation(pair_key, groups)
    marks = jnp.zeros((groups, groups), jnp.float32).at[jnp.arange(groups), pairing].set(1.0)
    marks = jnp.maximum(marks, marks.T)
    factor = 1.0 + 3.0 * marks
    values = (values.reshape(groups, tile, groups, tile) * factor[:, None, :, None]).reshape(M, M)
    values = jnp.clip(values, -16.0, 16.0)
    return (values * M ** (-0.5)).astype(jnp.float32)


def block_levels(rng, extent, split, smallest, largest):
    loudness = 1.0
    for position, blocks in split:
        heights = jax.random.uniform(jax.random.fold_in(jax.random.fold_in(rng, 6), position), (blocks,), jnp.float32, smallest / len(split), largest / len(split))
        loudness = loudness * jnp.repeat(jnp.exp(heights), extent[position] // blocks).reshape((-1,) + (1,) * (len(extent) - 1 - position))
    return loudness


def normal_values(key, extent, deviation, bound, pieces=(), held_as=jnp.bfloat16):
    result = deviation * jax.random.normal(key, extent, jnp.float32)
    if pieces:
        result = result * block_levels(key, extent, pieces, -0.22, 0.18)
    return jnp.clip(result, -bound, bound).astype(held_as)


def setup_inputs(seed: int = 0) -> dict:
    arg_keys = jax.random.split(jax.random.key(seed), 9)
    return {
        "inverse_block": draw_inverse_block(jax.random.fold_in(arg_keys[8], 71), 0),
        "grid_position": jax.random.permutation(arg_keys[1], M).astype(jnp.int32),
        "panel_a": normal_values(arg_keys[2], (W, M), 0.25, 1.5, ((0, 4), (1, 8)), jnp.float32),
        "pivot_inverse_a": normal_values(arg_keys[3], (W, W), 1.0, 6.0, (), jnp.float32),
        "chosen_rows": draw_chosen_rows(jax.random.fold_in(arg_keys[8], 71), 0),
        "top_panel_b": normal_values(arg_keys[5], (W, W), 0.25, 1.5, (), jnp.float32),
        "panel_b": normal_values(arg_keys[6], (W, MB), 0.25, 1.5, ((0, 4), (1, 8)), jnp.float32),
        "pivot_inverse_b": normal_values(arg_keys[7], (W, W), 1.0, 6.0, (), jnp.float32),
    }


def spread(panel_t, positions, order):
    return jnp.zeros((order, panel_t.shape[0]), jnp.float32).at[positions].set(panel_t.T)


def reference(inverse_block, grid_position, panel_a, pivot_inverse_a, chosen_rows, top_panel_b, panel_b, pivot_inverse_b):
    exact = lax.Precision.HIGHEST
    order = inverse_block.shape[0]
    full_a = spread(panel_a, grid_position, order)
    inverse_panel_a = -jnp.dot(inverse_block, full_a, precision=exact, preferred_element_type=jnp.float32)
    diagonal_a = pivot_inverse_a - jnp.dot(full_a.T, inverse_panel_a, precision=exact, preferred_element_type=jnp.float32)
    positions_b = grid_position[chosen_rows]
    full_b = spread(panel_b, positions_b, order)
    selected = jnp.zeros((order,), jnp.float32).at[positions_b].set(1.0)
    cross = jnp.dot(inverse_panel_a.T, full_b, precision=exact, preferred_element_type=jnp.float32)
    inverse_top_b = -(jnp.dot(diagonal_a, top_panel_b, precision=exact, preferred_element_type=jnp.float32) + cross)
    bottom = jnp.dot(inverse_block, full_b, precision=exact, preferred_element_type=jnp.float32)
    bottom = bottom + jnp.dot(inverse_panel_a, top_panel_b, precision=exact, preferred_element_type=jnp.float32)
    inverse_panel_b = -bottom * selected[:, None]
    diagonal_b = pivot_inverse_b - jnp.dot(top_panel_b.T, inverse_top_b, precision=exact, preferred_element_type=jnp.float32)
    diagonal_b = diagonal_b - jnp.dot(full_b.T, inverse_panel_b, precision=exact, preferred_element_type=jnp.float32)
    return inverse_panel_a, diagonal_a, inverse_panel_b, inverse_top_b, diagonal_b
```

```python
import functools
import math

import jax
import jax.numpy as jnp
from jax import lax
from jax.experimental import pallas as pl
from jax.experimental.pallas import tpu as pltpu
from jax.sharding import PartitionSpec as P


BLOCK = 128
MIB = 1 << 20


def call(kernel, outs, scalars, arrays, scratch=(), flops=0, limit=24):
    moved = sum(a.size * 4 for a in arrays) + sum(math.prod(s) * 4 for s, _ in outs)
    return pl.pallas_call(
        kernel,
        out_shape=[jax.ShapeDtypeStruct(s, d) for s, d in outs],
        in_specs=[pl.BlockSpec(memory_space=pltpu.SMEM)] * len(scalars)
        + [pl.BlockSpec(memory_space=pltpu.VMEM)] * len(arrays),
        out_specs=[pl.BlockSpec(memory_space=pltpu.VMEM)] * len(outs),
        scratch_shapes=list(scratch),
        compiler_params=pltpu.CompilerParams(vmem_limit_bytes=limit * MIB),
        cost_estimate=pl.CostEstimate(flops=flops, bytes_accessed=moved, transcendentals=0),
    )(*scalars, *arrays)


F32 = jnp.float32
BF16 = jnp.bfloat16


def halves(x):
    hi = x.astype(BF16)
    return hi, (x - hi.astype(F32)).astype(BF16)


def thirds(x):
    hi = x.astype(BF16)
    rest = x - hi.astype(F32)
    mid = rest.astype(BF16)
    return hi, mid, (rest - mid.astype(F32)).astype(BF16)


def mm(a, b, dims):
    return lax.dot_general(a, b, (dims, ((), ())), preferred_element_type=F32)


NN = ((1,), (0,))
NT = ((1,), (1,))
TN = ((0,), (0,))


def dot3(a, b, dims=NN):
    ah, al = a if isinstance(a, tuple) else halves(a)
    bh, bl = b if isinstance(b, tuple) else halves(b)
    return mm(ah, bh, dims) + (mm(ah, bl, dims) + mm(al, bh, dims))


def position_kernel(grid_ref, chosen_ref, out_ref):
    grid = grid_ref[...]
    chosen = chosen_ref[...]
    groups, count = grid.shape[0], chosen.shape[1]
    high = (grid >> 7).astype(F32).astype(BF16)
    low = (grid & 127).astype(F32).astype(BF16)
    row = lax.broadcasted_iota(jnp.int32, (groups, count), 0)
    hot = jnp.where(row == (chosen >> 7), 1.0, 0.0).astype(BF16)
    values = mm(high, hot, TN) * 128.0 + mm(low, hot, TN)
    lane = lax.broadcasted_iota(jnp.int32, (BLOCK, count), 0)
    picked = jnp.where(lane == (chosen & 127), values, 0.0)
    out_ref[...] = jnp.sum(picked, axis=0, keepdims=True).astype(jnp.int32)


def select_kernel(n_row, n_col, cols_here, rows_here, own_rows, with_valid, ids_ref, pos_ref, *refs):
    chunks, outs = refs[:n_col], refs[n_col:]
    row, col = ids_ref[0], ids_ref[1]
    width, length = chunks[0].shape
    starts = [(col * cols_here, cols_here)]
    for d in range(n_row):
        peer = lax.rem(row + d, n_row)
        starts.append((peer * rows_here + col * own_rows, own_rows))
    target = jnp.concatenate(
        [s + lax.broadcasted_iota(jnp.int32, (n, 1), 0) for s, n in starts], axis=0
    )
    total = None
    for j in range(n_col):
        source = jnp.bitwise_xor(col, j)
        pos = pos_ref[:, pl.ds(pl.multiple_of(source * length, BLOCK), length)]
        hot = jnp.where(pos == target, 1.0, 0.0).astype(BF16)
        parts = jnp.concatenate(thirds(chunks[j][...]), axis=0)
        term = mm(hot, parts, NT)
        total = term if total is None else total + term
    value = (total[:, :width] + total[:, width : 2 * width]) + total[:, 2 * width :]
    at = 0
    for i, (_, n) in enumerate(starts):
        outs[i][...] = value[at : at + n]
        at += n
    if with_valid:
        own = starts[1][0] + lax.broadcasted_iota(jnp.int32, (own_rows, 1), 0)
        found = jnp.where(pos_ref[...] == own, 1.0, 0.0)
        hit = jnp.sum(found, axis=1, keepdims=True)
        outs[-1][...] = jnp.broadcast_to(hit, outs[-1].shape)


def product_kernel(n_row, n_chip, own_rows, ids_ref, near_ref, far_ref, *refs):
    near, far = refs[:n_row], refs[n_row : 2 * n_row]
    outs, slots = refs[2 * n_row : -1], refs[-1]
    row, col = ids_ref[0], ids_ref[1]
    chip, core = col >> 1, col & 1
    cols = near_ref.shape[1]
    for d in range(n_row):
        source = lax.rem(row + n_row - d, n_row)
        slots[source, :cols, :] = near[d][...]
        slots[source, cols:, :] = far[d][...]
    right = halves(jnp.concatenate([slots[w] for w in range(n_row)], axis=1))
    left = []
    for m in range(n_chip):
        to = jnp.bitwise_xor(chip, m)
        here = near_ref[pl.ds(pl.multiple_of((2 * to + core) * own_rows, 8), own_rows), :]
        left.append(jnp.concatenate([here, far_ref[to]], axis=1))
    out = dot3(jnp.concatenate(left, axis=0), right)
    for m in range(n_chip):
        outs[m][...] = out[m * own_rows : (m + 1) * own_rows]


def own_kernel(n_row, ids_ref, *refs):
    a, b, out_ref, slots = refs[:n_row], refs[n_row : 2 * n_row], refs[-2], refs[-1]
    row = ids_ref[0]
    for d in range(n_row):
        source = lax.rem(row + n_row - d, n_row)
        slots[source] = a[d][...]
        slots[n_row + source] = b[d][...]
    out_ref[...] = jnp.concatenate([slots[w] for w in range(2 * n_row)], axis=1)


def form_kernel(n_chip, n_block, n_left, n_right, ids_ref, table_ref, *refs):
    left, right = refs[:n_left], refs[n_left : n_left + n_right]
    outs = refs[n_left + n_right : -5]
    lh, ll, rh, rl, z = refs[-5:]
    chip, core = ids_ref[1] >> 1, ids_ref[1] & 1
    at = 0
    rows = left[0].shape[0]

    def stack(group):
        pairs = [
            jnp.concatenate([group[i][...], group[i + 1][...]], axis=0)
            for i in range(0, len(group), 2)
        ]
        return jnp.concatenate(pairs, axis=1)

    lh[...], ll[...] = (x.T for x in halves(stack(left)))
    rh[...], rl[...] = halves(stack(right))
    for b in range(n_block):
        i = pl.multiple_of(table_ref[(core * n_block + b) * 2] * BLOCK, BLOCK)
        j = pl.multiple_of(table_ref[(core * n_block + b) * 2 + 1] * BLOCK, BLOCK)
        z[b * BLOCK : (b + 1) * BLOCK, :] = dot3(
            (lh[pl.ds(i, BLOCK), :], ll[pl.ds(i, BLOCK), :]),
            (rh[:, pl.ds(j, BLOCK)], rl[:, pl.ds(j, BLOCK)]),
        )
    size = outs[0].shape[0]
    for m in range(n_chip):
        to = jnp.bitwise_xor(chip, m)
        outs[m][...] = z[pl.ds(pl.multiple_of(to * size, 8), size), :]


def plane_sum_kernel(n_row, n_chip, ids_ref, *refs):
    parts, outs, total = refs[:n_chip], refs[n_chip:-1], refs[-1]
    row = ids_ref[0]
    value = parts[0][...]
    for m in range(1, n_chip):
        value = value + parts[m][...]
    total[...] = value
    size = outs[0].shape[0]
    for d in range(n_row):
        to = lax.rem(row + d, n_row)
        outs[d][...] = total[pl.ds(pl.multiple_of(to * size, 8), size), :]


def place(ids_ref, n_row, n_chip, near, far, z):
    row, chip, core = ids_ref[0], ids_ref[1] >> 1, ids_ref[1] & 1
    size = near[0].shape[0] // n_row
    for group, side in ((near, core), (far, 1 - core)):
        for m in range(n_chip):
            slab = side * n_chip + jnp.bitwise_xor(chip, m)
            for d in range(n_row):
                source = lax.rem(row + n_row - d, n_row)
                start = pl.multiple_of((slab * n_row + source) * size, 8)
                z[pl.ds(start, size), :] = group[m][d * size : (d + 1) * size, :]


def symmetric(z, base, n):
    block = {}
    at = base
    for i in range(n):
        for j in range(i, n):
            x = z[at * BLOCK : (at + 1) * BLOCK, :]
            block[i, j] = x
            if i != j:
                block[j, i] = x.T
            at += 1
    rows = [jnp.concatenate([block[i, j] for j in range(n)], axis=1) for i in range(n)]
    return jnp.concatenate(rows, axis=0)


def first_kernel(n_row, n_chip, ids_ref, pivot_ref, top_ref, *refs):
    near, far = refs[:n_chip], refs[n_chip : 2 * n_chip]
    diag_ref, out_ref, rest_ref, z = refs[2 * n_chip :]
    place(ids_ref, n_row, n_chip, near, far, z)
    n = top_ref.shape[0] // BLOCK
    diag = pivot_ref[...] + symmetric(z, 0, n)
    diag_ref[...] = diag
    base = n * (n + 1) // 2
    rows = []
    for i in range(n):
        at = [(base + i * n + j) * BLOCK for j in range(n)]
        rows.append(jnp.concatenate([z[a : a + BLOCK, :] for a in at], axis=1))
    cross = jnp.concatenate(rows, axis=0)
    top = top_ref[...]
    inverse_top = cross - dot3(diag, top)
    out_ref[...] = inverse_top
    left = jnp.concatenate([top, cross], axis=0)
    right = jnp.concatenate([inverse_top, top], axis=0)
    rest_ref[...] = dot3(halves(left.T), right)


def second_kernel(n_row, n_chip, ids_ref, pivot_ref, rest_ref, *refs):
    near, far = refs[:n_chip], refs[n_chip : 2 * n_chip]
    diag_ref, z = refs[2 * n_chip :]
    place(ids_ref, n_row, n_chip, near, far, z)
    n = pivot_ref.shape[0] // BLOCK
    diag_ref[...] = (pivot_ref[...] - rest_ref[...]) + symmetric(z, 0, n)


def lower_kernel(ya_ref, yb_ref, top_ref, valid_ref, out_ref):
    bottom = yb_ref[...] - dot3(ya_ref[...], top_ref[...])
    out_ref[...] = jnp.where(valid_ref[:, :1] > 0.0, -bottom, 0.0)


def body(
    inverse_block,
    grid_position,
    panel_a,
    pivot_inverse_a,
    chosen_rows,
    top_panel_b,
    panel_b,
    pivot_inverse_b,
):
    n_row, n_col = lax.axis_size("row"), lax.axis_size("col")
    n_chip = n_col // 2
    n_dev = n_row * n_col
    row, col = lax.axis_index("row"), lax.axis_index("col")
    ids = jnp.stack([row, col]).astype(jnp.int32)
    core = lax.rem(col, 2)
    rows_here, cols_here = inverse_block.shape
    own_rows = rows_here // n_col
    width = top_panel_b.shape[0]
    n_side = width // BLOCK
    order = grid_position.shape[0]
    count = chosen_rows.shape[0]
    slice_width = panel_a.shape[0]

    def across(x, mask):
        return lax.ppermute(x, "col", [(i, i ^ mask) for i in range(n_col)])

    def along(x, d):
        return lax.ppermute(x, "row", [(i, (i + d) % n_row) for i in range(n_row)])

    def gather_plane(x):
        same = [x] + [across(x, 2 * m) for m in range(1, n_chip)]
        out = []
        for s in same:
            out += [s, across(s, 1)]
        return out

    chunks_a = gather_plane(panel_a)
    chunks_b = gather_plane(panel_b)
    by_parity = inverse_block.reshape(n_chip, 2, own_rows, cols_here)
    far_block = across(lax.dynamic_index_in_dim(by_parity, 1 - core, 1, keepdims=False), 1)

    pos_a = grid_position.reshape(1, order)
    (pos_b,) = call(
        position_kernel,
        [((1, count), jnp.int32)],
        (),
        (grid_position.reshape(order // BLOCK, BLOCK), chosen_rows.reshape(1, count)),
        flops=order * count * 4,
    )

    def select(chunks, pos, with_valid):
        outs = [((cols_here, slice_width), F32)] + [((own_rows, slice_width), F32)] * n_row
        if with_valid:
            outs.append(((own_rows, BLOCK), F32))
        return call(
            functools.partial(
                select_kernel, n_row, n_col, cols_here, rows_here, own_rows, with_valid
            ),
            outs,
            (ids,),
            (pos, *chunks),
            flops=6 * pos.shape[1] * (cols_here + n_row * own_rows) * slice_width,
        )

    def product(mine):
        near = [mine] + [along(mine, d) for d in range(1, n_row)]
        far = [across(x, 1) for x in near]
        return near, far

    def multiply(near, far):
        out = call(
            functools.partial(product_kernel, n_row, n_chip, own_rows),
            [((own_rows, width), F32)] * n_chip,
            (ids,),
            (inverse_block, far_block, *near, *far),
            scratch=[pltpu.VMEM((n_row, 2 * cols_here, slice_width), F32)],
            flops=6 * rows_here * cols_here * width,
            limit=40,
        )
        total = out[0]
        for m in range(1, n_chip):
            total = total + across(out[m], 2 * m)
        return total

    mine_a, *rows_a = select(chunks_a, pos_a, False)
    near_a, far_a = product(mine_a)
    mine_b, *rows_b = select(chunks_b, pos_b, True)
    valid = rows_b.pop()
    near_b, far_b = product(mine_b)

    rows_a = [rows_a[0]] + [along(rows_a[d], d) for d in range(1, n_row)]
    rows_b = [rows_b[0]] + [along(rows_b[d], d) for d in range(1, n_row)]
    (own,) = call(
        functools.partial(own_kernel, n_row),
        [((own_rows, 2 * width), F32)],
        (ids,),
        (*rows_a, *rows_b),
        scratch=[pltpu.VMEM((2 * n_row, own_rows, slice_width), F32)],
    )
    pair = across(own, 1)
    own_a, own_b = own[:, :width], own[:, width:]
    pair_a, pair_b = pair[:, :width], pair[:, width:]

    def reduce_blocks(table, left, right):
        unit = math.lcm(8 * n_dev, 2 * BLOCK)
        total = -(-len(table) * BLOCK // unit) * unit
        half = total // 2
        n_block = half // BLOCK
        full = table + [(0, 0)] * (2 * n_block - len(table))
        flat = jnp.array([v for ij in full for v in ij], dtype=jnp.int32)
        size = half // n_chip
        wide_l = sum(x.shape[1] for x in left[::2])
        wide_r = sum(x.shape[1] for x in right[::2])
        out = call(
            functools.partial(form_kernel, n_chip, n_block, len(left), len(right)),
            [((size, BLOCK), F32)] * n_chip,
            (ids, flat),
            (*left, *right),
            scratch=[
                pltpu.VMEM((wide_l, 2 * own_rows), BF16),
                pltpu.VMEM((wide_l, 2 * own_rows), BF16),
                pltpu.VMEM((2 * own_rows, wide_r), BF16),
                pltpu.VMEM((2 * own_rows, wide_r), BF16),
                pltpu.VMEM((half, BLOCK), F32),
            ],
            flops=6 * half * BLOCK * 2 * own_rows,
        )
        parts = [out[0]] + [across(out[m], 2 * m) for m in range(1, n_chip)]
        cut = call(
            functools.partial(plane_sum_kernel, n_row, n_chip),
            [((size // n_row, BLOCK), F32)] * n_row,
            (ids,),
            parts,
            scratch=[pltpu.VMEM((size, BLOCK), F32)],
        )
        total_here = cut[0]
        for d in range(1, n_row):
            total_here = total_here + along(cut[d], d)
        line = jnp.concatenate(
            [total_here] + [along(total_here, d) for d in range(1, n_row)], axis=0
        )
        near = [line] + [across(line, 2 * m) for m in range(1, n_chip)]
        far = [across(x, 1) for x in near]
        return near, far, pltpu.VMEM((total, BLOCK), F32)

    upper = [(i, j) for i in range(n_side) for j in range(i, n_side)]
    product_a = multiply(near_a, far_a)
    pair_product_a = across(product_a, 1)
    table = upper + [(n_side + i, n_side + j) for i in range(n_side) for j in range(n_side)]
    near, far, room = reduce_blocks(
        table,
        (own_a, pair_a, product_a, pair_product_a),
        (product_a, pair_product_a, own_b, pair_b),
    )
    diagonal_a, inverse_top_b, rest = call(
        functools.partial(first_kernel, n_row, n_chip),
        [((width, width), F32)] * 3,
        (ids,),
        (pivot_inverse_a, top_panel_b, *near, *far),
        scratch=[room],
        flops=18 * width**3,
    )

    product_b = multiply(near_b, far_b)
    pair_product_b = across(product_b, 1)
    near, far, room = reduce_blocks(
        upper, (own_b, pair_b), (product_b, pair_product_b)
    )
    (inverse_panel_b,) = call(
        lower_kernel,
        [((own_rows, width), F32)],
        (),
        (product_a, product_b, top_panel_b, valid),
        flops=6 * own_rows * width**2,
    )
    (diagonal_b,) = call(
        functools.partial(second_kernel, n_row, n_chip),
        [((width, width), F32)],
        (ids,),
        (pivot_inverse_b, rest, *near, *far),
        scratch=[room],
    )
    return (-product_a, diagonal_a, inverse_panel_b, inverse_top_b, diagonal_b)


def solution(mesh):
    in_specs = (P("row", "col"), P(), P("row", "col"), P(), P(), P(), P("row", "col"), P())
    out_specs = (P(("row", "col"), None), P(), P(("row", "col"), None), P(), P())
    return jax.shard_map(body, mesh=mesh, in_specs=in_specs, out_specs=out_specs, check_vma=False)
```
